128 devices in a mesh: node: 32 (over y, x, core), rhs: 4 (over z).
Axes of the slice: x: 4, y: 4, z: 4, core: 2. Of those that a mesh axis runs over, the one named last changes fastest.
Arguments:
- right_side: float32 [64, 5, 256, 128], P('rhs', None, 'node'), may hold values from -6 to 6
- diag_tiles: bfloat16 [5, 256, 128, 128], P(None, ('node', 'rhs')), may hold values from -0.25 to 1.65
- off_tiles: bfloat16 [4, 256, 4, 128, 128], P(None, ('node', 'rhs')), may hold values from -0.125 to 0.125
- src_part: int32 [4, 256, 4], P(None, 'node'), may hold values from 0 to 31, all different within a row; in each aligned block of 8 rows (0 to 7, 8 to 15, ..., all dimensions but the last counted through in order) at most 2 rows name the same one
- src_slot: int32 [4, 256, 4], P(None, 'node'), may hold values from 0 to 7
Outputs:
- solution: float32 [64, 5, 256, 128], P('rhs', None, 'node')
The draws below stay inside these ranges and needn't reach their ends.
Inputs may be any that keep to these rules, and one draw needn't show every extreme that they name: `src_part`: over the 8 block rows of one partition at one level, each row names 4 different partitions, and no partition is named by more than 2 rows.
All inputs are finite; a program needn't handle non-finite values.
Results may differ from the reference program's by a relative error of at most 0.006.
Values may be sent and summed in bfloat16 or wider, within the bound.
A program may use at most 64 MiB of HBM per device.

```python
import math
import jax
import jax.numpy as jnp
import numpy as np
from jax import lax

S = 128
RHS = 64
K = 4
LEVELS = 5
BLK = 8
NB = 256
CAP = 2
N_NODE = 32


def draw_diag_tiles(key, part):
    first_key, second_key = jax.random.split(jax.random.fold_in(key, 7))
    shape = (LEVELS, NB, S, S)
    identity = jnp.eye(S, dtype=jnp.float32)
    scales = jax.random.uniform(first_key, (LEVELS, NB, S, 1), jnp.float32, 0.6, 1.2)
    noise = jnp.clip(jax.random.normal(second_key, shape, jnp.float32), -4.0, 4.0) * 0.35 * S ** (-0.5)
    return (identity * scales + noise).astype(jnp.bfloat16)


def place_ends(drawn, rng, smallest, top_value):
    shape = drawn.shape
    index_at = [jax.random.randint(jax.random.fold_in(rng, axis), (), 0, shape[axis]) for axis in range(len(shape))]
    drawn = drawn.at[tuple(index_at)].set(smallest)
    longest = shape.index(max(shape))
    index_at[longest] = (index_at[longest] + 1) % shape[longest]
    return drawn.at[tuple(index_at)].set(top_value)


def level_of(rng, dims, shards, least, high):
    def one(position, blocks):
        steps = jax.random.uniform(jax.random.fold_in(jax.random.fold_in(rng, 6), position), (blocks,), jnp.float32, least / len(shards), high / len(shards))
        return jnp.repeat(jnp.exp(steps), dims[position] // blocks).reshape((-1,) + (1,) * (len(dims) - position - 1))

    loudness = one(*shards[0])
    for cut in shards[1:]:
        loudness = loudness * one(*cut)
    return loudness


def deal_out(rng, own, number, rows, amount, top, limit, slope):
    ranking = jax.random.permutation(rng, amount)
    packed, ordinary = portions_of(amount, rows * top, limit, slope, True), portions_of(amount, rows * top, limit, slope, False)
    places = jnp.arange(amount)

    def named(lengths, turn):
        used = int((lengths > 0).sum())
        fixed = max(1, used // 4)
        passed = fixed + (places - fixed + turn * (used - fixed)) % max(1, amount - fixed)
        return jnp.zeros((amount,), jnp.int32).at[ranking[jnp.where(places < fixed, places, passed)]].set(jnp.asarray(lengths, jnp.int32))

    lengths = jnp.where(number % 4 == 0, named(packed, number // 4), named(ordinary, number - number // 4 - 1))
    mixed = jax.random.permutation(jax.random.fold_in(own, 3), amount)
    source_of, sink = mixed[0:amount // 2 * 2:2], mixed[1:amount // 2 * 2:2]
    room = jnp.minimum(lengths[source_of] - 1, limit - lengths[sink]) // 2
    room = jnp.where((source_of == ranking[0]) | (sink == ranking[0]) | (lengths[sink] == 0), 0, jnp.maximum(room, 0))
    passed = jax.random.randint(jax.random.fold_in(own, 4), (amount // 2,), 0, 1 << 20) % (room + 1)
    lengths = lengths.at[source_of].add(-passed).at[sink].add(passed)
    members = jnp.searchsorted(jnp.cumsum(lengths), jnp.arange(rows * top), side="right").astype(jnp.int32)
    listing = members.reshape(top, rows).T
    listing = listing[jax.random.permutation(jax.random.fold_in(own, 1), rows)]
    turn = jax.random.randint(jax.random.fold_in(own, 2), (rows, 1), 0, top)
    return jnp.take_along_axis(listing, (jnp.arange(top)[None, :] + turn) % top, axis=1)


def portions_of(amount, total, most, lean, full):
    weights = [(1 << 20) // math.isqrt(rank ** lean) + 1 for rank in range(1, amount + 1)]
    largest = most if full else min(most, max(-(-total // amount), total * weights[0] // sum(weights)))
    least = 1 if total - largest >= amount - 1 else 0
    holding, rest = [largest] + [least] * (amount - 1), total - largest - least * (amount - 1)
    while rest > 0:
        candidates = [i for i in range(1, amount) if holding[i] < largest] or [i for i in range(1, amount) if holding[i] < most]
        whole, remaining = sum([weights[i] for i in candidates]), rest
        for i in candidates:
            more = min(most - holding[i], max(1, remaining * weights[i] // whole), rest)
            holding[i] = holding[i] + more
            rest = rest - more
    return np.array(holding)


def centred(key, extent, deviation, bound, shards=(), kind=jnp.bfloat16):
    entries = jax.random.normal(key, extent, jnp.float32) * deviation
    if len(shards) > 0:
        entries = level_of(key, extent, shards, -0.22, 0.18) * entries
    return jnp.clip(entries, min=-bound, max=bound).astype(kind)


def setup_inputs(seed: int = 0) -> dict:
    keys = jax.random.split(jax.random.key(seed), 6)
    right_side = centred(keys[0], (RHS, LEVELS, NB, S), 1.0, 6.0, ((0, 4), (2, 32)), jnp.float32)
    diag_tiles = draw_diag_tiles(jax.random.fold_in(keys[5], 71), 0)
    off_tiles = centred(keys[2], (LEVELS - 1, NB, K, S, S), (4 * S * K) ** -0.5, 0.125, ((1, 128),))
    src_part_keys = jax.random.split(jax.random.fold_in(keys[3], 1), (LEVELS - 1) * NB // BLK)
    src_part_turns = jax.random.permutation(jax.random.fold_in(keys[3], 3), (LEVELS - 1) * NB // BLK)
    src_part = jax.vmap(lambda own, number: deal_out(jax.random.fold_in(keys[3], 2), own, number, BLK, N_NODE, K, CAP, 2))(src_part_keys, src_part_turns).reshape((LEVELS - 1, NB, K))
    src_slot = place_ends(jax.random.randint(keys[4], (LEVELS - 1, NB, K), 0, BLK), jax.random.fold_in(keys[4], 1), 0, BLK - 1).astype(jnp.int32)
    return {"right_side": right_side, "diag_tiles": diag_tiles, "off_tiles": off_tiles, "src_part": src_part, "src_slot": src_slot}


def reference(right_side, diag_tiles, off_tiles, src_part, src_slot):
    coupled_block = (src_part * BLK + src_slot).astype(jnp.int32)
    stored = []
    previous = None
    for level_at in range(LEVELS):
        current = right_side[:, level_at]
        if level_at > 0:
            picked = jnp.take(previous, coupled_block[level_at - 1].reshape(-1), axis=1)
            picked = picked.reshape(RHS, NB, K, S).astype(jnp.float32)
            coupled = jnp.einsum("cnks,nkts->cnt", picked, off_tiles[level_at - 1].astype(jnp.float32))
            current = current - coupled
        rounded = lax.optimization_barrier(current.astype(jnp.bfloat16)).astype(jnp.float32)
        previous = jnp.einsum("cns,nts->cnt", rounded, diag_tiles[level_at].astype(jnp.float32)).astype(jnp.bfloat16)
        stored.append(previous)
    results = [None] * LEVELS
    upper_round = None
    for level_at in range(LEVELS - 1, -1, -1):
        incoming = jnp.zeros((RHS, NB, S), jnp.float32)
        if level_at < LEVELS - 1:
            contrib_terms = jnp.einsum("cnt,nkts->cnks", upper_round, off_tiles[level_at].astype(jnp.float32))
            incoming = incoming.at[:, coupled_block[level_at].reshape(-1)].add(contrib_terms.reshape(RHS, NB * K, S))
        back_in = (stored[level_at].astype(jnp.float32) - incoming).astype(jnp.bfloat16)
        back_in = lax.optimization_barrier(back_in).astype(jnp.float32)
        solution = jnp.einsum("cns,nst->cnt", back_in, diag_tiles[level_at].astype(jnp.float32))
        upper_round = lax.optimization_barrier(solution.astype(jnp.bfloat16)).astype(jnp.float32)
        results[level_at] = solution
    return jnp.stack(results, axis=1)
```

```python
import functools

import jax
import jax.numpy as jnp
from jax import lax
from jax.experimental import pallas as pl
from jax.experimental.pallas import tpu as pltpu
from jax.sharding import PartitionSpec as P

MESH = pl.DeviceIdType.MESH
XS = 4
YS = 4
CORES = 2
CAP = 2


def dot_nt(a, b):
    return lax.dot_general(a, b, (((1,), (1,)), ((), ())), preferred_element_type=jnp.float32)


def dot_nn(a, b):
    return lax.dot_general(a, b, (((1,), (0,)), ((), ())), preferred_element_type=jnp.float32)


def kernel(dims, pos, inv, req_out, rs_hbm, diag_hbm, off_hbm, out_hbm, *scratch):
    columns, levels, rows, size, fanout, nodes, ranks = dims
    own = rows // ranks
    links = levels - 1
    scratch = list(scratch)
    take = lambda count: [scratch.pop(0) for _ in range(count)]
    rs_v, out_v, diag_v, off_v, contrib, req_in = take(6)
    solved = take(levels)
    send_f, recv_f, send_b, recv_b = take(links), take(links), take(links), take(links)
    (req_s,) = take(1)
    (local_sem, out_sem, req_send, req_recv, xy_send, xy_recv, z_send, z_recv) = take(8)

    me = lax.axis_index("node")
    my_z = lax.axis_index("rhs")
    my_y, my_x, my_c = me // (XS * CORES), (me // CORES) % XS, me % CORES
    up, down = (my_z + 1) % ranks, (my_z + ranks - 1) % ranks
    far = (my_z + 2) % ranks

    def partner(s):
        dy, dx, dc = s // (XS * CORES), (s // CORES) % XS, s % CORES
        y, x, c = (my_y + dy) % YS, (my_x + dx) % XS, (my_c + dc) % CORES
        back = ((YS - dy) % YS) * (XS * CORES) + ((XS - dx) % XS) * CORES + dc
        return (y * XS + x) * CORES + c, back

    mine = pl.ds(own * my_z, own)
    local = [pltpu.make_async_copy(rs_hbm, rs_v, local_sem.at[0])]
    local += [pltpu.make_async_copy(diag_hbm, diag_v.at[:, mine], local_sem.at[1])]
    local += [pltpu.make_async_copy(off_hbm, off_v.at[:, mine], local_sem.at[2])]
    local += [pltpu.make_async_copy(req_out.at[0], req_in.at[0], local_sem.at[3])]
    for copy in local:
        copy.start()

    barrier = pltpu.get_barrier_semaphore()

    def greet(s, carry):
        node, _ = partner(s)
        pl.semaphore_signal(barrier, inc=1, device_id={"node": node}, device_id_type=MESH)
        return carry

    lax.fori_loop(1, nodes, greet, 0)
    for z in (up, down):
        pl.semaphore_signal(barrier, inc=1, device_id={"rhs": z}, device_id_type=MESH)
    pl.semaphore_wait(barrier, nodes + 1)

    def piece(level):
        return [(0, level)] + ([(1, level - 1)] if level else [])

    def tile_copy(kind, level, way, hop):
        sem = (kind * levels + level) * 4 + way * 2 + hop
        whole = off_v if kind else diag_v
        target = up if way == 0 else down
        if hop == 0:
            src = (off_hbm if kind else diag_hbm).at[level]
            dst = whole.at[level, mine]
        else:
            origin = down if way == 0 else up
            span = pl.ds(own * origin + way * (own // 2), own // 2)
            src = whole.at[level, span]
            dst = whole.at[level, span]
        return pltpu.make_async_remote_copy(
            src_ref=src, dst_ref=dst, send_sem=z_send.at[sem], recv_sem=z_recv.at[sem],
            device_id={"rhs": target}, device_id_type=MESH)

    def send_tiles(level, hop):
        for kind, at in piece(level):
            for way in (0, 1):
                tile_copy(kind, at, way, hop).start()

    def arrived(level, hop):
        for kind, at in piece(level):
            for way in (0, 1):
                tile_copy(kind, at, way, hop).wait_recv()

    def request_copy(s):
        node, back = partner(s)
        return pltpu.make_async_remote_copy(
            src_ref=req_out.at[s], dst_ref=req_in.at[back], send_sem=req_send, recv_sem=req_recv,
            device_id={"node": node}, device_id_type=MESH)

    def ask(s, carry):
        request_copy(s).start()
        return carry

    send_tiles(0, 0)
    lax.fori_loop(1, nodes, ask, 0)
    send_tiles(1, 0)

    others = pl.ds(1, nodes - 1)

    def wait_all(ref, sem):
        pltpu.make_async_copy(ref, ref, sem).wait()

    def exchange(source, table, buffers, received, turn):
        def one(s, carry):
            for j in range(CAP):
                buffers[s, j] = source[table(s, j)]
            node, back = partner(s)
            pltpu.make_async_remote_copy(
                src_ref=buffers.at[s], dst_ref=received.at[back], send_sem=xy_send.at[turn],
                recv_sem=xy_recv.at[turn], device_id={"node": node}, device_id_type=MESH).start()
            return carry

        lax.fori_loop(1, nodes, one, 0)
        for j in range(CAP):
            received[0, j] = source[table(0, j)]

    arrived(0, 0)
    send_tiles(0, 1)
    send_tiles(2, 0)
    for copy in local:
        copy.wait()
    wait_all(req_in.at[others], req_recv)
    to_scalars = pltpu.make_async_copy(req_in, req_s, local_sem.at[4])
    to_scalars.start()
    arrived(0, 1)

    stride = levels * rows
    for level in range(levels):
        if level:
            link = level - 1
            arrived(level, 0)
            send_tiles(level, 1)
            if level + 2 < levels:
                send_tiles(level + 2, 0)
            wait_all(recv_f[link].at[others], xy_recv.at[link])
            arrived(level, 1)
        for n in range(rows):
            current = rs_v[pl.ds(level * rows + n, columns, stride), :]
            if level:
                coupled = None
                for k in range(fanout):
                    at = pos[link, n * fanout + k]
                    term = dot_nt(recv_f[link][at // CAP, at % CAP], off_v[link, n, k])
                    coupled = term if coupled is None else coupled + term
                current = current - coupled
            rounded = current.astype(jnp.bfloat16)
            solved[level][n] = dot_nt(rounded, diag_v[level, n]).astype(jnp.bfloat16)
        if level == 0:
            to_scalars.wait()
        if level < levels - 1:
            exchange(solved[level], lambda s, j: req_s[s, 0, level * CAP + j],
                     send_f[level], recv_f[level], level)

    contrib[rows * fanout] = jnp.zeros((columns, size), jnp.bfloat16)
    outs = []
    for level in range(levels - 1, -1, -1):
        if level < levels - 1:
            wait_all(recv_b[level].at[others], xy_recv.at[links + level])

            def gather(s, sums):
                sums = list(sums)
                for j in range(CAP):
                    value = recv_b[level][s, j].astype(jnp.float32)
                    row = req_s[s, 0, level * CAP + j]
                    for m in range(rows):
                        sums[m] = sums[m] + value * jnp.where(row == m, 1.0, 0.0)
                return tuple(sums)

            zero = jnp.zeros((columns, size), jnp.float32)
            incoming = lax.fori_loop(0, nodes, gather, (zero,) * rows)
        for m in range(rows):
            if level < levels - 1:
                back_in = (solved[level][m].astype(jnp.float32) - incoming[m]).astype(jnp.bfloat16)
            else:
                back_in = solved[level][m]
            answer = dot_nn(back_in, diag_v[level, m])
            out_v[pl.ds(level * rows + m, columns, stride), :] = answer
            if level:
                rounded = answer.astype(jnp.bfloat16)
                for k in range(fanout):
                    contrib[m * fanout + k] = dot_nn(rounded, off_v[level - 1, m, k]).astype(jnp.bfloat16)
        if level:
            link = level - 1
            exchange(contrib, lambda s, j: inv[link, s * CAP + j], send_b[link], recv_b[link], links + link)

    final = pltpu.make_async_copy(out_v, out_hbm, out_sem)
    final.start()
    wait_all(req_out.at[others], req_send)
    for link in range(links):
        wait_all(send_f[link].at[others], xy_send.at[link])
        wait_all(send_b[link].at[others], xy_send.at[links + link])
    for level in range(levels):
        for kind, at in piece(level):
            for way in (0, 1):
                for hop in (0, 1):
                    tile_copy(kind, at, way, hop).wait_send()
    final.wait()


def tables(src_part, src_slot, nodes):
    links, rows, fanout = src_part.shape
    count = rows * fanout
    part = src_part.reshape(links, count)
    slot = src_slot.reshape(links, count)
    me = lax.axis_index("node")
    dy = (part // (XS * CORES) - me // (XS * CORES)) % YS
    dx = ((part // CORES) % XS - (me // CORES) % XS) % XS
    dc = (part - me) % CORES
    relative = (dy * XS + dx) * CORES + dc
    order = jnp.arange(count, dtype=jnp.int32)
    same = (part[:, :, None] == part[:, None, :]) & (order[None, None, :] < order[None, :, None])
    pos = relative * CAP + same.sum(-1).astype(jnp.int32)
    hit = pos[:, None, :] == jnp.arange(nodes * CAP, dtype=jnp.int32)[None, :, None]
    want = jnp.where(hit, slot[:, None, :], 0).sum(-1)
    inv = count + jnp.where(hit, order[None, None, :] - count, 0).sum(-1)
    want = want.reshape(links, nodes, CAP).transpose(1, 0, 2).reshape(nodes, 1, links * CAP)
    want = jnp.pad(want, ((0, 0), (0, 0), (0, 128 - links * CAP)))
    return pos.astype(jnp.int32), inv.astype(jnp.int32), want.astype(jnp.int32)


def on_device(right_side, diag_tiles, off_tiles, src_part, src_slot):
    columns, levels, rows, size = right_side.shape
    links, own, fanout = off_tiles.shape[:3]
    nodes, ranks = lax.axis_size("node"), lax.axis_size("rhs")
    pos, inv, want = tables(src_part, src_slot, nodes)
    dims = (columns, levels, rows, size, fanout, nodes, ranks)
    bf16 = jnp.bfloat16
    pieces = 2 * levels
    block = (columns, size)
    scratch = [
        pltpu.VMEM((columns * levels * rows, size), jnp.float32),
        pltpu.VMEM((columns * levels * rows, size), jnp.float32),
        pltpu.VMEM((levels, rows, size, size), bf16),
        pltpu.VMEM((links, rows, fanout, size, size), bf16),
        pltpu.VMEM((rows * fanout + 1,) + block, bf16),
        pltpu.VMEM((nodes, 1, 128), jnp.int32),
    ]
    scratch += [pltpu.VMEM((rows,) + block, bf16)] * levels
    scratch += [pltpu.VMEM((nodes, CAP) + block, bf16)] * (4 * links)
    scratch += [
        pltpu.SMEM((nodes, 1, 128), jnp.int32),
        pltpu.SemaphoreType.DMA((5,)),
        pltpu.SemaphoreType.DMA,
        pltpu.SemaphoreType.DMA,
        pltpu.SemaphoreType.DMA,
        pltpu.SemaphoreType.DMA((2 * links,)),
        pltpu.SemaphoreType.DMA((2 * links,)),
        pltpu.SemaphoreType.DMA((pieces * 4,)),
        pltpu.SemaphoreType.DMA((pieces * 4,)),
    ]
    smem = pl.BlockSpec(memory_space=pltpu.SMEM)
    vmem = pl.BlockSpec(memory_space=pltpu.VMEM)
    hbm = pl.BlockSpec(memory_space=pl.ANY)
    out = pl.pallas_call(
        functools.partial(kernel, dims),
        out_shape=jax.ShapeDtypeStruct((columns * levels * rows, size), jnp.float32),
        in_specs=[smem, smem, vmem, hbm, hbm, hbm],
        out_specs=hbm,
        scratch_shapes=scratch,
        compiler_params=pltpu.CompilerParams(
            collective_id=0, has_side_effects=True, vmem_limit_bytes=48 * 2**20),
    )(pos, inv, want, right_side.reshape(columns * levels * rows, size), diag_tiles, off_tiles)
    return out.reshape(columns, levels, rows, size)


def solution(mesh):
    placed = (
        P("rhs", None, "node", None),
        P(None, ("node", "rhs"), None, None),
        P(None, ("node", "rhs"), None, None, None),
        P(None, "node", None),
        P(None, "node", None),
    )
    return jax.shard_map(
        on_device,
        mesh=mesh,
        in_specs=placed,
        out_specs=P("rhs", None, "node", None),
        check_vma=False,
    )
```

```python
import functools

import jax
import jax.numpy as jnp
from jax import lax
from jax.experimental import pallas as pl
from jax.experimental.pallas import tpu as pltpu
from jax.sharding import PartitionSpec as P

MESH = pl.DeviceIdType.MESH
XS = 4
YS = 4
CORES = 2
CAP = 2


def dot_nt(a, b):
    return lax.dot_general(a, b, (((1,), (1,)), ((), ())), preferred_element_type=jnp.float32)


def dot_nn(a, b):
    return lax.dot_general(a, b, (((1,), (0,)), ((), ())), preferred_element_type=jnp.float32)


def split(s):
    return s // (XS * CORES), (s // CORES) % XS, s % CORES


def opposite(s):
    dy, dx, dc = split(s)
    return ((YS - dy) % YS) * (XS * CORES) + ((XS - dx) % XS) * CORES + dc


def hops(s):
    dy, dx, dc = split(s)
    return min(dy, YS - dy) + min(dx, XS - dx)


ORDER = sorted(range(1, YS * XS * CORES), key=lambda s: (-hops(s), -s))


def kernel(dims, part_hbm, slot_hbm, rs_hbm, diag_hbm, off_hbm, out_v, *scratch):
    columns, levels, rows, size, fanout, nodes, ranks = dims
    own = rows // ranks
    links = levels - 1
    stride = levels * rows
    scratch = list(scratch)
    take = lambda count: [scratch.pop(0) for _ in range(count)]
    rs_v, diag_v, off_v, contrib, req_out, req_in, own_tab = take(7)
    solved = take(levels)
    send_f, recv_f, send_b, recv_b = take(links), take(links), take(links), take(links)
    part_s, slot_s, req_s, own_s = take(4)
    (local_sem, req_send, req_recv, xy_send, xy_recv, z_send, z_recv) = take(7)

    me = lax.axis_index("node")
    my_z = lax.axis_index("rhs")
    my_y, my_x, my_c = me // (XS * CORES), (me // CORES) % XS, me % CORES
    up, down = (my_z + 1) % ranks, (my_z + ranks - 1) % ranks
    at_y = [((my_y + d) % YS) * (XS * CORES) for d in range(YS)]
    at_x = [((my_x + d) % XS) * CORES for d in range(XS)]
    at_c = [(my_c + d) % CORES for d in range(CORES)]

    def partner(s):
        dy, dx, dc = split(s)
        return at_y[dy] + at_x[dx] + at_c[dc]

    barrier = pltpu.get_barrier_semaphore()
    for s in ORDER:
        pl.semaphore_signal(barrier, inc=1, device_id={"node": partner(s)}, device_id_type=MESH)
    for z in (up, down):
        pl.semaphore_signal(barrier, inc=1, device_id={"rhs": z}, device_id_type=MESH)

    mine = pl.ds(own * my_z, own)
    index_in = [pltpu.make_async_copy(part_hbm, part_s, local_sem.at[0]),
                pltpu.make_async_copy(slot_hbm, slot_s, local_sem.at[1])]
    local = [pltpu.make_async_copy(diag_hbm, diag_v.at[:, mine], local_sem.at[2]),
             pltpu.make_async_copy(rs_hbm, rs_v, local_sem.at[3]),
             pltpu.make_async_copy(off_hbm, off_v.at[:, mine], local_sem.at[4])]
    for copy in index_in + local:
        copy.start()

    for copy in index_in:
        copy.wait()
    count = rows * fanout
    lane = lax.broadcasted_iota(jnp.int32, (1, links * nodes), 1)
    there = lane & (nodes - 1)
    lane_y, lane_x, lane_c = there >> 3, (there >> 1) & 3, there & 1
    lane_key = (lane - there) + (((lane_y + my_y) & 3) << 3) + (((lane_x + my_x) & 3) << 1) + ((lane_c + my_c) & 1)

    def entry(i):
        level, at = i // count, i % count
        row, k = at // fanout, at % fanout
        return level * nodes + part_s[level, k, row], slot_s[level, k, row], at

    def collect(i, carry):
        first, second, keys = carry
        key, slot, at = entry(i)
        value = at * rows + slot
        hit = lane_key == key
        fresh = first < 0
        second = jnp.where(hit & (first >= 0), value, second)
        first = jnp.where(hit & fresh, value, first)
        return first, second, jnp.where(lane == i, key, keys)

    none = jnp.full((1, links * nodes), -1, jnp.int32)
    first, second, keys = lax.fori_loop(0, links * count, collect, (none, none, none), unroll=4)

    def earlier(i, ranks_of):
        key, _, _ = entry(i)
        return ranks_of + jnp.where((keys == key) & (lane > i), 1, 0)

    rank = lax.fori_loop(0, links * count, earlier, jnp.zeros((1, links * nodes), jnp.int32), unroll=4)
    rel_y, rel_x, rel_c = ((keys & 31) >> 3) - my_y, ((keys >> 1) & 3) - my_x, (keys & 1) - my_c
    own_tab[0:1, :] = ((((rel_y & 3) << 3) + ((rel_x & 3) << 1) + (rel_c & 1)) << 1) + jnp.minimum(rank, CAP - 1)
    own_tab[1:2, :] = jnp.where(first < 0, count, first >> 3)
    own_tab[2:3, :] = jnp.where(second < 0, count, second >> 3)
    asked = jnp.where(first < 0, 0, first & 7) + (jnp.where(second < 0, 0, second & 7) << 3)
    req_out[...] = asked
    req_in[0] = asked

    pl.semaphore_wait(barrier, nodes + 1)

    def tile_copy(kind, level, way, step):
        sem = ((kind * levels + level) * 2 + way) * 3 + step
        whole = off_v if kind else diag_v
        at = level - kind
        target = up if way == 0 else down
        if step < 2:
            row = way if step == 0 else 1 - way
            src = (off_hbm if kind else diag_hbm).at[at, row]
            dst = whole.at[at, own * my_z + row]
        else:
            origin = down if way == 0 else up
            src = dst = whole.at[at, own * origin + way]
        return pltpu.make_async_remote_copy(
            src_ref=src, dst_ref=dst, send_sem=z_send.at[sem], recv_sem=z_recv.at[sem],
            device_id={"rhs": target}, device_id_type=MESH)

    def pieces(level):
        return [(kind, way) for kind in range(1 + (level > 0)) for way in (0, 1)]

    def send_tiles(level, step):
        if level < levels:
            for kind, way in pieces(level):
                tile_copy(kind, level, way, step).start()

    def arrived(level, step):
        for kind, way in pieces(level):
            tile_copy(kind, level, way, step).wait_recv()

    others = pl.ds(1, nodes - 1)

    def wait_all(ref, sem):
        pltpu.make_async_copy(ref, ref, sem).wait()

    def exchange(blocks, buffers, received, turn):
        for j in range(CAP):
            received[0, j] = blocks(0, j)
        for s in ORDER:
            for j in range(CAP):
                buffers[s, j] = blocks(s, j)
            pltpu.make_async_remote_copy(
                src_ref=buffers.at[s], dst_ref=received.at[opposite(s)], send_sem=xy_send.at[turn],
                recv_sem=xy_recv.at[turn], device_id={"node": partner(s)}, device_id_type=MESH).start()

    def wanted(s, link):
        both = req_s[s, 0, link * nodes + opposite(s)]
        return lax.rem(both, rows), lax.div(both, rows)

    send_tiles(0, 0)
    send_tiles(0, 1)
    for s in ORDER:
        pltpu.make_async_remote_copy(
            src_ref=req_out, dst_ref=req_in.at[opposite(s)], send_sem=req_send, recv_sem=req_recv,
            device_id={"node": partner(s)}, device_id_type=MESH).start()
    send_tiles(1, 0)
    to_scalars = [pltpu.make_async_copy(own_tab, own_s, local_sem.at[0]),
                  pltpu.make_async_copy(req_in, req_s, local_sem.at[1])]
    to_scalars[0].start()
    arrived(0, 0)
    send_tiles(0, 2)
    send_tiles(1, 1)
    for copy in local:
        copy.wait()
    arrived(0, 1)
    arrived(0, 2)

    for level in range(levels):
        link = level - 1
        if level:
            wait_all(recv_f[link].at[others], xy_recv.at[link])
            arrived(level, 1)
            arrived(level, 2)
        for n in range(rows):
            current = rs_v[pl.ds(level * rows + n, columns, stride), :]
            if level:
                picked = []
                for k in range(fanout):
                    at = own_s[0, link * count + n * fanout + k]
                    picked.append(recv_f[link][lax.div(at, CAP), lax.rem(at, CAP)])
                tiles = jnp.concatenate([off_v[link, n, k] for k in range(fanout)], axis=1)
                current = current - dot_nt(jnp.concatenate(picked, axis=1), tiles)
            solved[level][n] = dot_nt(current.astype(jnp.bfloat16), diag_v[level, n]).astype(jnp.bfloat16)
        if level == 0:
            wait_all(req_in.at[others], req_recv)
            to_scalars[1].start()
            for copy in to_scalars:
                copy.wait()
        if level < links:
            exchange(lambda s, j: solved[level][wanted(s, level)[j]], send_f[level], recv_f[level], level)
            arrived(level + 1, 0)
            send_tiles(level + 1, 2)
            send_tiles(level + 2, 0)
            send_tiles(level + 2, 1)

    contrib[count] = jnp.zeros((columns, size), jnp.bfloat16)
    for level in range(levels - 1, -1, -1):
        link = level - 1
        if level < links:
            wait_all(recv_b[level].at[others], xy_recv.at[links + level])

            def gather(s, sums):
                sums = list(sums)
                for j in range(CAP):
                    value = recv_b[level][s, j].astype(jnp.float32)
                    row = rows_of[s][j]
                    for m in range(rows):
                        sums[m] = sums[m] + value * jnp.where(row == m, 1.0, 0.0)
                return tuple(sums)

            rows_of = [wanted(s, level) for s in range(nodes)]
            incoming = (jnp.zeros((columns, size), jnp.float32),) * rows
            for s in range(nodes):
                incoming = gather(s, incoming)
        for m in range(rows):
            if level < links:
                back_in = (solved[level][m].astype(jnp.float32) - incoming[m]).astype(jnp.bfloat16)
            else:
                back_in = solved[level][m]
            answer = dot_nn(back_in, diag_v[level, m])
            out_v[pl.ds(level * rows + m, columns, stride), :] = answer
            if level:
                tiles = jnp.concatenate([off_v[link, m, k] for k in range(fanout)], axis=1)
                products = dot_nn(answer.astype(jnp.bfloat16), tiles).astype(jnp.bfloat16)
                for k in range(fanout):
                    contrib[m * fanout + k] = products[:, k * size:(k + 1) * size]
        if level:
            exchange(lambda s, j: contrib[own_s[1 + j, link * nodes + s]], send_b[link], recv_b[link], links + link)

    for s in ORDER:
        wait_all(req_in.at[s], req_send)
    for link in range(links):
        wait_all(send_f[link].at[others], xy_send.at[link])
        wait_all(send_b[link].at[others], xy_send.at[links + link])
    for level in range(levels):
        for kind, way in pieces(level):
            for step in range(3):
                tile_copy(kind, level, way, step).wait_send()


def on_device(right_side, diag_tiles, off_tiles, src_part, src_slot):
    columns, levels, rows, size = right_side.shape
    links, own, fanout = off_tiles.shape[:3]
    nodes, ranks = lax.axis_size("node"), lax.axis_size("rhs")
    dims = (columns, levels, rows, size, fanout, nodes, ranks)
    bf16 = jnp.bfloat16
    block = (columns, size)
    lanes = links * nodes
    scratch = [
        pltpu.VMEM((columns * levels * rows, size), jnp.float32),
        pltpu.VMEM((levels, rows, size, size), bf16),
        pltpu.VMEM((links, rows, fanout, size, size), bf16),
        pltpu.VMEM((rows * fanout + 1,) + block, bf16),
        pltpu.VMEM((1, lanes), jnp.int32),
        pltpu.VMEM((nodes, 1, lanes), jnp.int32),
        pltpu.VMEM((8, lanes), jnp.int32),
    ]
    scratch += [pltpu.VMEM((rows,) + block, bf16)] * levels
    scratch += [pltpu.VMEM((nodes, CAP) + block, bf16)] * (4 * links)
    scratch += [
        pltpu.SMEM((links, fanout, rows), jnp.int32),
        pltpu.SMEM((links, fanout, rows), jnp.int32),
        pltpu.SMEM((nodes, 1, lanes), jnp.int32),
        pltpu.SMEM((8, lanes), jnp.int32),
        pltpu.SemaphoreType.DMA((5,)),
        pltpu.SemaphoreType.DMA,
        pltpu.SemaphoreType.DMA,
        pltpu.SemaphoreType.DMA((2 * links,)),
        pltpu.SemaphoreType.DMA((2 * links,)),
        pltpu.SemaphoreType.DMA((levels * 12,)),
        pltpu.SemaphoreType.DMA((levels * 12,)),
    ]
    hbm = pl.BlockSpec(memory_space=pltpu.MemorySpace.HBM)
    out = pl.pallas_call(
        functools.partial(kernel, dims),
        out_shape=jax.ShapeDtypeStruct((columns * levels * rows, size), jnp.float32),
        in_specs=[hbm] * 5,
        out_specs=pl.BlockSpec(memory_space=pltpu.VMEM),
        scratch_shapes=scratch,
        compiler_params=pltpu.CompilerParams(
            collective_id=0, has_side_effects=True, vmem_limit_bytes=67043328),
    )(src_part.transpose(0, 2, 1), src_slot.transpose(0, 2, 1),
      right_side.reshape(columns * levels * rows, size), diag_tiles, off_tiles)
    return out.reshape(columns, levels, rows, size)


def solution(mesh):
    placed = (
        P("rhs", None, "node", None),
        P(None, ("node", "rhs"), None, None),
        P(None, ("node", "rhs"), None, None, None),
        P(None, "node", None),
        P(None, "node", None),
    )
    return jax.shard_map(
        on_device,
        mesh=mesh,
        in_specs=placed,
        out_specs=P("rhs", None, "node", None),
        check_vma=False,
    )
```

```python
import functools

import jax
import jax.numpy as jnp
from jax import lax
from jax.experimental import pallas as pl
from jax.experimental.pallas import tpu as pltpu
from jax.sharding import PartitionSpec as P

MESH = pl.DeviceIdType.MESH
XS = 4
YS = 4
CORES = 2
CAP = 2


def dot_nt(a, b):
    return lax.dot_general(a, b, (((1,), (1,)), ((), ())), preferred_element_type=jnp.float32)


def dot_nn(a, b):
    return lax.dot_general(a, b, (((1,), (0,)), ((), ())), preferred_element_type=jnp.float32)


def split(s):
    return s // (XS * CORES), (s // CORES) % XS, s % CORES


def opposite(s):
    dy, dx, dc = split(s)
    return ((YS - dy) % YS) * (XS * CORES) + ((XS - dx) % XS) * CORES + dc


def hops(s):
    dy, dx, dc = split(s)
    return min(dy, YS - dy) + min(dx, XS - dx)


ORDER = sorted(range(1, YS * XS * CORES), key=lambda s: (-hops(s), -s))
ROW = [s for s in ORDER if split(s)[0] == 0]
COLUMN = [s for s in ORDER if split(s)[1:] == (0, 0)]


def kernel(dims, part_hbm, slot_hbm, rs_hbm, diag_hbm, off_hbm, out_v, *scratch):
    columns, levels, rows, size, fanout, nodes, ranks = dims
    own = rows // ranks
    links = levels - 1
    stride = levels * rows
    scratch = list(scratch)
    take = lambda count: [scratch.pop(0) for _ in range(count)]
    rs_v, diag_v, off_v, contrib, req_out, req_in, own_tab = take(7)
    solved = take(links)
    send_f, recv_f, send_b, recv_b = take(links), take(links), take(links), take(links)
    part_s, slot_s, req_s, own_s = take(4)
    (entered, local_sem, req_send, req_recv, xy_send, xy_recv, z_send, z_recv) = take(8)

    me = lax.axis_index("node")
    my_z = lax.axis_index("rhs")
    my_y, my_x, my_c = me // (XS * CORES), (me // CORES) % XS, me % CORES
    up, down = (my_z + 1) % ranks, (my_z + ranks - 1) % ranks
    at_y = [((my_y + d) % YS) * (XS * CORES) for d in range(YS)]
    at_x = [((my_x + d) % XS) * CORES for d in range(XS)]
    at_c = [(my_c + d) % CORES for d in range(CORES)]

    def partner(s):
        dy, dx, dc = split(s)
        return at_y[dy] + at_x[dx] + at_c[dc]

    barrier = pltpu.get_barrier_semaphore()
    for s in ROW + COLUMN:
        pl.semaphore_signal(barrier, inc=1, device_id={"node": partner(s)}, device_id_type=MESH)
    for z in (up, down):
        pl.semaphore_signal(barrier, inc=1, device_id={"rhs": z}, device_id_type=MESH)

    mine = pl.ds(own * my_z, own)
    index_in = [pltpu.make_async_copy(part_hbm, part_s, local_sem.at[0]),
                pltpu.make_async_copy(slot_hbm, slot_s, local_sem.at[1])]
    for copy in index_in:
        copy.start()

    def tile_copy(kind, level, way, step):
        sem = ((kind * levels + level) * 2 + way) * 3 + step
        whole = off_v if kind else diag_v
        at = level - kind
        target = up if way == 0 else down
        if step < 2:
            row = way if step == 0 else 1 - way
            src = (off_hbm if kind else diag_hbm).at[at, row]
            dst = whole.at[at, own * my_z + row]
        else:
            origin = down if way == 0 else up
            src = dst = whole.at[at, own * origin + way]
        return pltpu.make_async_remote_copy(
            src_ref=src, dst_ref=dst, send_sem=z_send.at[sem], recv_sem=z_recv.at[sem],
            device_id={"rhs": target}, device_id_type=MESH)

    def pieces(level):
        return [(kind, way) for kind in range(1 + (level > 0)) for way in (0, 1)]

    def send_tiles(level, step):
        if level < levels:
            for kind, way in pieces(level):
                tile_copy(kind, level, way, step).start()

    def arrived(level, step):
        for kind, way in pieces(level):
            tile_copy(kind, level, way, step).wait_recv()

    pl.semaphore_wait(barrier, len(ROW + COLUMN) + 2)
    send_tiles(0, 0)
    send_tiles(0, 1)
    for s in COLUMN:
        pl.semaphore_signal(entered, inc=1, device_id={"node": partner(s)}, device_id_type=MESH)
    send_tiles(1, 0)
    local = [pltpu.make_async_copy(diag_hbm, diag_v.at[:, mine], local_sem.at[2]),
             pltpu.make_async_copy(rs_hbm, rs_v, local_sem.at[3]),
             pltpu.make_async_copy(off_hbm, off_v.at[:, mine], local_sem.at[4])]
    for copy in local:
        copy.start()

    for copy in index_in:
        copy.wait()
    count = rows * fanout
    lane = lax.broadcasted_iota(jnp.int32, (1, links * nodes), 1)
    there = lane & (nodes - 1)
    lane_y, lane_x, lane_c = there >> 3, (there >> 1) & 3, there & 1
    lane_key = (lane - there) + (((lane_y + my_y) & 3) << 3) + (((lane_x + my_x) & 3) << 1) + ((lane_c + my_c) & 1)

    def entry(i):
        level, at = i // count, i % count
        row, k = at // fanout, at % fanout
        return level * nodes + part_s[level, k, row], slot_s[level, k, row], at

    def collect(i, carry):
        first, second, keys = carry
        key, slot, at = entry(i)
        value = at * rows + slot
        hit = lane_key == key
        fresh = first < 0
        second = jnp.where(hit & (first >= 0), value, second)
        first = jnp.where(hit & fresh, value, first)
        return first, second, jnp.where(lane == i, key, keys)

    none = jnp.full((1, links * nodes), -1, jnp.int32)
    first, second, keys = lax.fori_loop(0, links * count, collect, (none, none, none), unroll=4)

    def earlier(i, ranks_of):
        key, _, _ = entry(i)
        return ranks_of + jnp.where((keys == key) & (lane > i), 1, 0)

    rank = lax.fori_loop(0, links * count, earlier, jnp.zeros((1, links * nodes), jnp.int32), unroll=4)
    rel_y, rel_x, rel_c = ((keys & 31) >> 3) - my_y, ((keys >> 1) & 3) - my_x, (keys & 1) - my_c
    own_tab[0:1, :] = ((((rel_y & 3) << 3) + ((rel_x & 3) << 1) + (rel_c & 1)) << 1) + jnp.minimum(rank, CAP - 1)
    own_tab[1:2, :] = jnp.where(first < 0, count, first >> 3)
    own_tab[2:3, :] = jnp.where(second < 0, count, second >> 3)
    asked = jnp.where(first < 0, 0, first & 7) + (jnp.where(second < 0, 0, second & 7) << 3)
    req_out[...] = asked
    req_in[0] = asked

    others = pl.ds(1, nodes - 1)

    def wait_all(ref, sem):
        pltpu.make_async_copy(ref, ref, sem).wait()

    def exchange(blocks, buffers, received, turn):
        for j in range(CAP):
            received[0, j] = blocks(0, j)
        for s in ORDER:
            for j in range(CAP):
                buffers[s, j] = blocks(s, j)
            pltpu.make_async_remote_copy(
                src_ref=buffers.at[s], dst_ref=received.at[opposite(s)], send_sem=xy_send.at[turn],
                recv_sem=xy_recv.at[turn], device_id={"node": partner(s)}, device_id_type=MESH).start()

    def wanted(s, link):
        both = req_s[s, 0, link * nodes + opposite(s)]
        return lax.rem(both, rows), lax.div(both, rows)

    pl.semaphore_wait(entered, len(COLUMN))
    for s in ORDER:
        pltpu.make_async_remote_copy(
            src_ref=req_out, dst_ref=req_in.at[opposite(s)], send_sem=req_send, recv_sem=req_recv,
            device_id={"node": partner(s)}, device_id_type=MESH).start()
    to_scalars = [pltpu.make_async_copy(own_tab, own_s, local_sem.at[0]),
                  pltpu.make_async_copy(req_in, req_s, local_sem.at[1])]
    to_scalars[0].start()
    arrived(0, 0)
    send_tiles(0, 2)
    send_tiles(1, 1)
    for copy in local:
        copy.wait()

    def forward(level, n):
        link = level - 1
        current = rs_v[pl.ds(level * rows + n, columns, stride), :]
        if level:
            picked = []
            for k in range(fanout):
                at = own_s[0, link * count + n * fanout + k]
                picked.append(recv_f[link][lax.div(at, CAP), lax.rem(at, CAP)])
            tiles = jnp.concatenate([off_v[link, n, k] for k in range(fanout)], axis=1)
            current = current - dot_nt(jnp.concatenate(picked, axis=1), tiles)
        return dot_nt(current.astype(jnp.bfloat16), diag_v[level, n]).astype(jnp.bfloat16)

    def backward(level, n, back_in):
        answer = dot_nn(back_in, diag_v[level, n])
        out_v[pl.ds(level * rows + n, columns, stride), :] = answer
        if level:
            tiles = jnp.concatenate([off_v[level - 1, n, k] for k in range(fanout)], axis=1)
            products = dot_nn(answer.astype(jnp.bfloat16), tiles).astype(jnp.bfloat16)
            for k in range(fanout):
                contrib[n * fanout + k] = products[:, k * size:(k + 1) * size]

    far = (my_z + 2) % ranks
    arrivals = [(own * my_z, own * my_z + 1), (own * down, own * up + 1), (own * down + 1, own * up),
                (own * far, own * far + 1)]
    contrib[count] = jnp.zeros((columns, size), jnp.bfloat16)
    for level in range(levels):
        if level:
            wait_all(recv_f[level - 1].at[others], xy_recv.at[level - 1])
        for turn, pair in enumerate(arrivals):
            if turn > 1:
                arrived(level, turn - 1)
            for n in pair:
                if level < links:
                    solved[level][n] = forward(level, n)
                else:
                    backward(level, n, forward(level, n))
        if level == 0:
            wait_all(req_in.at[others], req_recv)
            to_scalars[1].start()
            for copy in to_scalars:
                copy.wait()
        if level < links:
            exchange(lambda s, j: solved[level][wanted(s, level)[j]], send_f[level], recv_f[level], level)
            arrived(level + 1, 0)
            send_tiles(level + 1, 2)
            send_tiles(level + 2, 0)
            send_tiles(level + 2, 1)

    for level in range(levels - 1, -1, -1):
        link = level - 1
        if level < links:
            wait_all(recv_b[level].at[others], xy_recv.at[links + level])

            def gather(s, sums):
                sums = list(sums)
                for j in range(CAP):
                    value = recv_b[level][s, j].astype(jnp.float32)
                    row = rows_of[s][j]
                    for m in range(rows):
                        sums[m] = sums[m] + value * jnp.where(row == m, 1.0, 0.0)
                return tuple(sums)

            rows_of = [wanted(s, level) for s in range(nodes)]
            incoming = (jnp.zeros((columns, size), jnp.float32),) * rows
            for s in range(nodes):
                incoming = gather(s, incoming)
            for m in range(rows):
                backward(level, m, (solved[level][m].astype(jnp.float32) - incoming[m]).astype(jnp.bfloat16))
        if level:
            exchange(lambda s, j: contrib[own_s[1 + j, link * nodes + s]], send_b[link], recv_b[link], links + link)

    for s in ORDER:
        wait_all(req_in.at[s], req_send)
    for link in range(links):
        wait_all(send_f[link].at[others], xy_send.at[link])
        wait_all(send_b[link].at[others], xy_send.at[links + link])
    for level in range(levels):
        for kind, way in pieces(level):
            for step in range(3):
                tile_copy(kind, level, way, step).wait_send()


def on_device(right_side, diag_tiles, off_tiles, src_part, src_slot):
    columns, levels, rows, size = right_side.shape
    links, own, fanout = off_tiles.shape[:3]
    nodes, ranks = lax.axis_size("node"), lax.axis_size("rhs")
    dims = (columns, levels, rows, size, fanout, nodes, ranks)
    bf16 = jnp.bfloat16
    block = (columns, size)
    lanes = links * nodes
    scratch = [
        pltpu.VMEM((columns * levels * rows, size), jnp.float32),
        pltpu.VMEM((levels, rows, size, size), bf16),
        pltpu.VMEM((links, rows, fanout, size, size), bf16),
        pltpu.VMEM((rows * fanout + 1,) + block, bf16),
        pltpu.VMEM((1, lanes), jnp.int32),
        pltpu.VMEM((nodes, 1, lanes), jnp.int32),
        pltpu.VMEM((8, lanes), jnp.int32),
    ]
    scratch += [pltpu.VMEM((rows,) + block, bf16)] * links
    scratch += [pltpu.VMEM((nodes, CAP) + block, bf16)] * (4 * links)
    scratch += [
        pltpu.SMEM((links, fanout, rows), jnp.int32),
        pltpu.SMEM((links, fanout, rows), jnp.int32),
        pltpu.SMEM((nodes, 1, lanes), jnp.int32),
        pltpu.SMEM((8, lanes), jnp.int32),
        pltpu.SemaphoreType.REGULAR,
        pltpu.SemaphoreType.DMA((5,)),
        pltpu.SemaphoreType.DMA,
        pltpu.SemaphoreType.DMA,
        pltpu.SemaphoreType.DMA((2 * links,)),
        pltpu.SemaphoreType.DMA((2 * links,)),
        pltpu.SemaphoreType.DMA((levels * 12,)),
        pltpu.SemaphoreType.DMA((levels * 12,)),
    ]
    hbm = pl.BlockSpec(memory_space=pltpu.MemorySpace.HBM)
    out = pl.pallas_call(
        functools.partial(kernel, dims),
        out_shape=jax.ShapeDtypeStruct((columns * levels * rows, size), jnp.float32),
        in_specs=[hbm] * 5,
        out_specs=pl.BlockSpec(memory_space=pltpu.VMEM),
        scratch_shapes=scratch,
        compiler_params=pltpu.CompilerParams(
            collective_id=0, has_side_effects=True, vmem_limit_bytes=67043328),
    )(src_part.transpose(0, 2, 1), src_slot.transpose(0, 2, 1),
      right_side.reshape(columns * levels * rows, size), diag_tiles, off_tiles)
    return out.reshape(columns, levels, rows, size)


def solution(mesh):
    placed = (
        P("rhs", None, "node", None),
        P(None, ("node", "rhs"), None, None),
        P(None, ("node", "rhs"), None, None, None),
        P(None, "node", None),
        P(None, "node", None),
    )
    return jax.shard_map(
        on_device,
        mesh=mesh,
        in_specs=placed,
        out_specs=P("rhs", None, "node", None),
        check_vma=False,
    )
```

```python
import functools

import jax
import jax.numpy as jnp
from jax import lax
from jax.experimental import pallas as pl
from jax.experimental.pallas import tpu as pltpu
from jax.sharding import PartitionSpec as P

MESH = pl.DeviceIdType.MESH
XS = 4
YS = 4
CORES = 2
CAP = 2


def dot_nt(a, b):
    return lax.dot_general(a, b, (((1,), (1,)), ((), ())), preferred_element_type=jnp.float32)


def dot_nn(a, b):
    return lax.dot_general(a, b, (((1,), (0,)), ((), ())), preferred_element_type=jnp.float32)


def split(s):
    return s // (XS * CORES), (s // CORES) % XS, s % CORES


def opposite(s):
    dy, dx, dc = split(s)
    return ((YS - dy) % YS) * (XS * CORES) + ((XS - dx) % XS) * CORES + dc


def hops(s):
    dy, dx, dc = split(s)
    return min(dy, YS - dy) + min(dx, XS - dx)


ORDER = sorted(range(1, YS * XS * CORES), key=lambda s: (-hops(s), -s))
ROW = [s for s in ORDER if split(s)[0] == 0]
COLUMN = [s for s in ORDER if split(s)[1:] == (0, 0)]


def kernel(dims, part_hbm, slot_hbm, rs_hbm, diag_hbm, off_hbm, out_hbm, *scratch):
    columns, levels, rows, size, fanout, nodes, ranks = dims
    own = rows // ranks
    links = levels - 1
    stride = levels * rows
    scratch = list(scratch)
    take = lambda count: [scratch.pop(0) for _ in range(count)]
    rs_v, out_v, diag_v, off_v, contrib, chosen, merged, req_out, req_in, own_tab = take(10)
    solved = take(links)
    send_f, recv_f, send_b, recv_b = take(links), take(links), take(links), take(links)
    part_s, slot_s, req_s, own_s = take(4)
    (entered, out_sem, local_sem, req_send, req_recv, xy_send, xy_recv, z_send, z_recv) = take(9)

    me = lax.axis_index("node")
    my_z = lax.axis_index("rhs")
    my_y, my_x, my_c = me // (XS * CORES), (me // CORES) % XS, me % CORES
    up, down = (my_z + 1) % ranks, (my_z + ranks - 1) % ranks
    at_y = [((my_y + d) % YS) * (XS * CORES) for d in range(YS)]
    at_x = [((my_x + d) % XS) * CORES for d in range(XS)]
    at_c = [(my_c + d) % CORES for d in range(CORES)]

    def partner(s):
        dy, dx, dc = split(s)
        return at_y[dy] + at_x[dx] + at_c[dc]

    barrier = pltpu.get_barrier_semaphore()
    for s in ROW + COLUMN:
        pl.semaphore_signal(barrier, inc=1, device_id={"node": partner(s)}, device_id_type=MESH)
    for z in (up, down):
        pl.semaphore_signal(barrier, inc=1, device_id={"rhs": z}, device_id_type=MESH)

    mine = pl.ds(own * my_z, own)
    index_in = [pltpu.make_async_copy(part_hbm, part_s, local_sem.at[0]),
                pltpu.make_async_copy(slot_hbm, slot_s, local_sem.at[1])]
    for copy in index_in:
        copy.start()

    def tile_copy(kind, level, way, step):
        sem = ((kind * levels + level) * 2 + way) * 3 + step
        whole = off_v if kind else diag_v
        at = level - kind
        target = up if way == 0 else down
        if step < 2:
            row = way if step == 0 else 1 - way
            src = (off_hbm if kind else diag_hbm).at[at, row]
            dst = whole.at[at, own * my_z + row]
        else:
            origin = down if way == 0 else up
            src = dst = whole.at[at, own * origin + way]
        return pltpu.make_async_remote_copy(
            src_ref=src, dst_ref=dst, send_sem=z_send.at[sem], recv_sem=z_recv.at[sem],
            device_id={"rhs": target}, device_id_type=MESH)

    def pieces(level):
        return [(kind, way) for kind in range(1 + (level > 0)) for way in (0, 1)]

    def send_tiles(level, step):
        if level < levels:
            for kind, way in pieces(level):
                tile_copy(kind, level, way, step).start()

    def arrived(level, step):
        for kind, way in pieces(level):
            tile_copy(kind, level, way, step).wait_recv()

    pl.semaphore_wait(barrier, len(ROW + COLUMN) + 2)
    send_tiles(0, 0)
    send_tiles(0, 1)
    for s in COLUMN:
        pl.semaphore_signal(entered, inc=1, device_id={"node": partner(s)}, device_id_type=MESH)
    send_tiles(1, 0)
    local = [pltpu.make_async_copy(diag_hbm, diag_v.at[:, mine], local_sem.at[2]),
             pltpu.make_async_copy(rs_hbm, rs_v, local_sem.at[3]),
             pltpu.make_async_copy(off_hbm, off_v.at[:, mine], local_sem.at[4])]
    for copy in local:
        copy.start()

    for copy in index_in:
        copy.wait()
    count = rows * fanout
    lane = lax.broadcasted_iota(jnp.int32, (1, links * nodes), 1)
    there = lane & (nodes - 1)
    lane_y, lane_x, lane_c = there >> 3, (there >> 1) & 3, there & 1
    lane_key = (lane - there) + (((lane_y + my_y) & 3) << 3) + (((lane_x + my_x) & 3) << 1) + ((lane_c + my_c) & 1)

    def entry(i):
        level, at = i // count, i % count
        row, k = at // fanout, at % fanout
        return level * nodes + part_s[level, k, row], slot_s[level, k, row], at

    def collect(i, carry):
        first, second, keys = carry
        key, slot, at = entry(i)
        value = at * rows + slot
        hit = lane_key == key
        fresh = first < 0
        second = jnp.where(hit & (first >= 0), value, second)
        first = jnp.where(hit & fresh, value, first)
        return first, second, jnp.where(lane == i, key, keys)

    none = jnp.full((1, links * nodes), -1, jnp.int32)
    first, second, keys = lax.fori_loop(0, links * count, collect, (none, none, none), unroll=4)

    def earlier(i, ranks_of):
        key, _, _ = entry(i)
        return ranks_of + jnp.where((keys == key) & (lane > i), 1, 0)

    rank = lax.fori_loop(0, links * count, earlier, jnp.zeros((1, links * nodes), jnp.int32), unroll=4)
    rel_y, rel_x, rel_c = ((keys & 31) >> 3) - my_y, ((keys >> 1) & 3) - my_x, (keys & 1) - my_c
    own_tab[0:1, :] = ((((rel_y & 3) << 3) + ((rel_x & 3) << 1) + (rel_c & 1)) << 1) + jnp.minimum(rank, CAP - 1)
    own_tab[1:2, :] = jnp.where(first < 0, count, first >> 3)
    own_tab[2:3, :] = jnp.where(second < 0, count, second >> 3)
    asked = jnp.where(first < 0, 0, first & 7) + (jnp.where(second < 0, 0, second & 7) << 3)
    req_out[...] = asked
    req_in[0] = asked

    others = pl.ds(1, nodes - 1)

    def wait_all(ref, sem):
        pltpu.make_async_copy(ref, ref, sem).wait()

    def exchange(blocks, buffers, received, turn):
        for j in range(CAP):
            received[0, j] = blocks(0, j)
        for s in ORDER:
            for j in range(CAP):
                buffers[s, j] = blocks(s, j)
            pltpu.make_async_remote_copy(
                src_ref=buffers.at[s], dst_ref=received.at[opposite(s)], send_sem=xy_send.at[turn],
                recv_sem=xy_recv.at[turn], device_id={"node": partner(s)}, device_id_type=MESH).start()

    def wanted(s, link):
        both = req_s[s, 0, link * nodes + opposite(s)]
        return lax.rem(both, rows), lax.div(both, rows)

    pl.semaphore_wait(entered, len(COLUMN))
    for s in ORDER:
        pltpu.make_async_remote_copy(
            src_ref=req_out, dst_ref=req_in.at[opposite(s)], send_sem=req_send, recv_sem=req_recv,
            device_id={"node": partner(s)}, device_id_type=MESH).start()
    to_scalars = [pltpu.make_async_copy(own_tab, own_s, local_sem.at[0]),
                  pltpu.make_async_copy(req_in, req_s, local_sem.at[1])]
    to_scalars[0].start()
    arrived(0, 0)
    send_tiles(0, 2)
    send_tiles(1, 1)
    for copy in local:
        copy.wait()

    def forward(level, n):
        link = level - 1
        current = rs_v[pl.ds(level * rows + n, columns, stride), :]
        if level:
            picked = []
            for k in range(fanout):
                at = own_s[0, link * count + n * fanout + k]
                picked.append(recv_f[link][lax.div(at, CAP), lax.rem(at, CAP)])
            tiles = jnp.concatenate([off_v[link, n, k] for k in range(fanout)], axis=1)
            current = current - dot_nt(jnp.concatenate(picked, axis=1), tiles)
        return dot_nt(current.astype(jnp.bfloat16), diag_v[level, n]).astype(jnp.bfloat16)

    def row_tiles(link, n):
        return jnp.concatenate([off_v[link, n, k] for k in range(fanout)], axis=1)

    def merge(level):
        for n in range(rows):
            merged[level - 1, n] = dot_nn(diag_v[level, n], row_tiles(level - 1, n)).astype(jnp.bfloat16)

    def answer_row(level, n, back_in):
        answer = dot_nn(back_in, diag_v[level, n])
        out_v[pl.ds(level * rows + n, columns, stride), :] = answer
        return answer.astype(jnp.bfloat16)

    def contribute(n, vector, tiles):
        products = dot_nn(vector, tiles).astype(jnp.bfloat16)
        for k in range(fanout):
            contrib[n * fanout + k] = products[:, k * size:(k + 1) * size]

    square = (rows * columns, size)
    of_row = lax.broadcasted_iota(jnp.int32, square, 0)
    of_lane = lax.broadcasted_iota(jnp.int32, square, 1)
    same_column = lax.rem(of_row, columns) == lax.rem(of_lane, columns)
    of_row = lax.div(of_row, columns)
    lane_block = lax.div(lax.broadcasted_iota(jnp.int32, (1, size), 1), columns)
    blocks = size // columns

    def choose(link):
        for start in range(0, nodes * CAP, blocks):
            owner = jnp.zeros((1, size), jnp.int32)
            for b in range(blocks):
                owner = jnp.where(lane_block == b, wanted((start + b) // CAP, link)[(start + b) % CAP], owner)
            hit = same_column & (of_row == owner)
            chosen[link, :, start * columns:start * columns + size] = jnp.where(hit, 1.0, 0.0).astype(jnp.bfloat16)

    far = (my_z + 2) % ranks
    arrivals = [(own * my_z, own * my_z + 1), (own * down, own * up + 1), (own * down + 1, own * up),
                (own * far, own * far + 1)]
    contrib[count] = jnp.zeros((columns, size), jnp.bfloat16)
    for level in range(levels):
        if level:
            wait_all(recv_f[level - 1].at[others], xy_recv.at[level - 1])
        for turn, pair in enumerate(arrivals):
            if turn > 1:
                arrived(level, turn - 1)
            for n in pair:
                if level < links:
                    solved[level][n] = forward(level, n)
                else:
                    contribute(n, answer_row(level, n, forward(level, n)), row_tiles(level - 1, n))
        if level == 0:
            wait_all(req_in.at[others], req_recv)
            to_scalars[1].start()
            for copy in to_scalars:
                copy.wait()
        if level < links:
            exchange(lambda s, j: solved[level][wanted(s, level)[j]], send_f[level], recv_f[level], level)
            arrived(level + 1, 0)
            send_tiles(level + 1, 2)
            send_tiles(level + 2, 0)
            send_tiles(level + 2, 1)
            choose(level)
            if level:
                merge(level)

    for level in range(levels - 1, -1, -1):
        link = level - 1
        if level < links:
            wait_all(recv_b[level].at[others], xy_recv.at[links + level])

            incoming = dot_nn(chosen[level], recv_b[level][...].reshape(nodes * CAP * columns, size))
            held = solved[level][...].reshape(rows * columns, size).astype(jnp.float32)
            back_in = (held - incoming).astype(jnp.bfloat16)
            back_rows = [back_in[m * columns:(m + 1) * columns] for m in range(rows)]
            if level:
                for m in range(rows):
                    contribute(m, back_rows[m], merged[link, m])
        if level:
            exchange(lambda s, j: contrib[own_s[1 + j, link * nodes + s]], send_b[link], recv_b[link], links + link)
        if level < links:
            for m in range(rows):
                answer_row(level, m, back_rows[m])
        for c in range(columns):
            span = pl.ds(c * stride + level * rows, rows)
            pltpu.make_async_copy(out_v.at[span], out_hbm.at[span], out_sem.at[level]).start()

    for level in range(levels):
        wait_all(out_v.at[pl.ds(0, columns * rows)], out_sem.at[level])
    for s in ORDER:
        wait_all(req_in.at[s], req_send)
    for link in range(links):
        wait_all(send_f[link].at[others], xy_send.at[link])
        wait_all(send_b[link].at[others], xy_send.at[links + link])
    for level in range(levels):
        for kind, way in pieces(level):
            for step in range(3):
                tile_copy(kind, level, way, step).wait_send()


def on_device(right_side, diag_tiles, off_tiles, src_part, src_slot):
    columns, levels, rows, size = right_side.shape
    links, own, fanout = off_tiles.shape[:3]
    nodes, ranks = lax.axis_size("node"), lax.axis_size("rhs")
    dims = (columns, levels, rows, size, fanout, nodes, ranks)
    bf16 = jnp.bfloat16
    block = (columns, size)
    lanes = links * nodes
    scratch = [
        pltpu.VMEM((columns * levels * rows, size), jnp.float32),
        pltpu.VMEM((columns * levels * rows, size), jnp.float32),
        pltpu.VMEM((levels, rows, size, size), bf16),
        pltpu.VMEM((links, rows, fanout, size, size), bf16),
        pltpu.VMEM((rows * fanout + 1,) + block, bf16),
        pltpu.VMEM((links, rows * columns, nodes * CAP * columns), bf16),
        pltpu.VMEM((links - 1, rows, size, fanout * size), bf16),
        pltpu.VMEM((1, lanes), jnp.int32),
        pltpu.VMEM((nodes, 1, lanes), jnp.int32),
        pltpu.VMEM((8, lanes), jnp.int32),
    ]
    scratch += [pltpu.VMEM((rows,) + block, bf16)] * links
    scratch += [pltpu.VMEM((nodes, CAP) + block, bf16)] * (4 * links)
    scratch += [
        pltpu.SMEM((links, fanout, rows), jnp.int32),
        pltpu.SMEM((links, fanout, rows), jnp.int32),
        pltpu.SMEM((nodes, 1, lanes), jnp.int32),
        pltpu.SMEM((8, lanes), jnp.int32),
        pltpu.SemaphoreType.REGULAR,
        pltpu.SemaphoreType.DMA((levels,)),
        pltpu.SemaphoreType.DMA((5,)),
        pltpu.SemaphoreType.DMA,
        pltpu.SemaphoreType.DMA,
        pltpu.SemaphoreType.DMA((2 * links,)),
        pltpu.SemaphoreType.DMA((2 * links,)),
        pltpu.SemaphoreType.DMA((levels * 12,)),
        pltpu.SemaphoreType.DMA((levels * 12,)),
    ]
    hbm = pl.BlockSpec(memory_space=pltpu.MemorySpace.HBM)
    out = pl.pallas_call(
        functools.partial(kernel, dims),
        out_shape=jax.ShapeDtypeStruct((columns * levels * rows, size), jnp.float32),
        in_specs=[hbm] * 5,
        out_specs=hbm,
        scratch_shapes=scratch,
        compiler_params=pltpu.CompilerParams(
            collective_id=0, has_side_effects=True, vmem_limit_bytes=67043328),
    )(src_part.transpose(0, 2, 1), src_slot.transpose(0, 2, 1),
      right_side.reshape(columns * levels * rows, size), diag_tiles, off_tiles)
    return out.reshape(columns, levels, rows, size)


def solution(mesh):
    placed = (
        P("rhs", None, "node", None),
        P(None, ("node", "rhs"), None, None),
        P(None, ("node", "rhs"), None, None, None),
        P(None, "node", None),
        P(None, "node", None),
    )
    return jax.shard_map(
        on_device,
        mesh=mesh,
        in_specs=placed,
        out_specs=P("rhs", None, "node", None),
        check_vma=False,
    )
```

```python
import functools

import jax
import jax.numpy as jnp
from jax import lax
from jax.experimental import pallas as pl
from jax.experimental.pallas import tpu as pltpu
from jax.sharding import PartitionSpec as P

MESH = pl.DeviceIdType.MESH
XS = 4
YS = 4
CORES = 2
CAP = 2


def dot_nt(a, b):
    return lax.dot_general(a, b, (((1,), (1,)), ((), ())), preferred_element_type=jnp.float32)


def dot_nn(a, b):
    return lax.dot_general(a, b, (((1,), (0,)), ((), ())), preferred_element_type=jnp.float32)


def split(s):
    return s // (XS * CORES), (s // CORES) % XS, s % CORES


def opposite(s):
    dy, dx, dc = split(s)
    return ((YS - dy) % YS) * (XS * CORES) + ((XS - dx) % XS) * CORES + dc


def hops(s):
    dy, dx, dc = split(s)
    return min(dy, YS - dy) + min(dx, XS - dx)


ORDER = sorted(range(1, YS * XS * CORES), key=lambda s: (-hops(s), -s))
ROW = [s for s in ORDER if split(s)[0] == 0]
COLUMN = [s for s in ORDER if split(s)[1:] == (0, 0)]


def kernel(dims, part_hbm, slot_hbm, rs_hbm, diag_hbm, off_hbm, out_hbm, *scratch):
    columns, levels, rows, size, fanout, nodes, ranks = dims
    own = rows // ranks
    links = levels - 1
    stride = levels * rows
    scratch = list(scratch)
    take = lambda count: [scratch.pop(0) for _ in range(count)]
    rs_v, out_v, diag_v, off_v, contrib, chosen, merged, req_out, req_in, own_tab = take(10)
    solved = take(links)
    send_f, recv_f, send_b, recv_b = take(links), take(links), take(links), take(links)
    part_s, slot_s, req_s, own_s = take(4)
    (entered, out_sem, local_sem, req_send, req_recv, xy_send, xy_recv, z_send, z_recv) = take(9)

    me = lax.axis_index("node")
    my_z = lax.axis_index("rhs")
    my_y, my_x, my_c = me // (XS * CORES), (me // CORES) % XS, me % CORES
    up, down = (my_z + 1) % ranks, (my_z + ranks - 1) % ranks
    at_y = [((my_y + d) % YS) * (XS * CORES) for d in range(YS)]
    at_x = [((my_x + d) % XS) * CORES for d in range(XS)]
    at_c = [(my_c + d) % CORES for d in range(CORES)]

    def partner(s):
        dy, dx, dc = split(s)
        return at_y[dy] + at_x[dx] + at_c[dc]

    barrier = pltpu.get_barrier_semaphore()
    for s in ROW + COLUMN:
        pl.semaphore_signal(barrier, inc=1, device_id={"node": partner(s)}, device_id_type=MESH)
    for z in (up, down):
        pl.semaphore_signal(barrier, inc=1, device_id={"rhs": z}, device_id_type=MESH)

    mine = pl.ds(own * my_z, own)
    index_in = [pltpu.make_async_copy(part_hbm, part_s, local_sem.at[0]),
                pltpu.make_async_copy(slot_hbm, slot_s, local_sem.at[1])]
    for copy in index_in:
        copy.start()

    def tile_copy(kind, level, way, step):
        sem = ((kind * levels + level) * 2 + way) * 3 + step
        whole = off_v if kind else diag_v
        at = level - kind
        target = up if way == 0 else down
        if step < 2:
            row = way if step == 0 else 1 - way
            src = (off_hbm if kind else diag_hbm).at[at, row]
            dst = whole.at[at, own * my_z + row]
        else:
            origin = down if way == 0 else up
            src = dst = whole.at[at, own * origin + way]
        return pltpu.make_async_remote_copy(
            src_ref=src, dst_ref=dst, send_sem=z_send.at[sem], recv_sem=z_recv.at[sem],
            device_id={"rhs": target}, device_id_type=MESH)

    def pieces(level):
        return [(kind, way) for kind in ((1, 0) if level else (0,)) for way in (0, 1)]

    def send_tiles(level, step):
        if level < levels:
            for kind, way in pieces(level):
                tile_copy(kind, level, way, step).start()

    def arrived(level, step, kinds=(0, 1)):
        for kind, way in pieces(level):
            if kind in kinds:
                tile_copy(kind, level, way, step).wait_recv()

    pl.semaphore_wait(barrier, len(ROW + COLUMN) + 2)
    send_tiles(0, 0)
    send_tiles(0, 1)
    for s in COLUMN:
        pl.semaphore_signal(entered, inc=1, device_id={"node": partner(s)}, device_id_type=MESH)
    send_tiles(1, 0)
    local = [pltpu.make_async_copy(diag_hbm, diag_v.at[:, mine], local_sem.at[2]),
             pltpu.make_async_copy(rs_hbm, rs_v, local_sem.at[3]),
             pltpu.make_async_copy(off_hbm, off_v.at[:, mine], local_sem.at[4])]
    for copy in local:
        copy.start()

    for copy in index_in:
        copy.wait()
    count = rows * fanout
    lane = lax.broadcasted_iota(jnp.int32, (1, links * nodes), 1)
    there = lane & (nodes - 1)
    lane_y, lane_x, lane_c = there >> 3, (there >> 1) & 3, there & 1
    lane_key = (lane - there) + (((lane_y + my_y) & 3) << 3) + (((lane_x + my_x) & 3) << 1) + ((lane_c + my_c) & 1)

    def entry(i):
        level, at = i // count, i % count
        row, k = at // fanout, at % fanout
        return level * nodes + part_s[level, k, row], slot_s[level, k, row], at

    def collect(i, carry):
        first, second, keys = carry
        key, slot, at = entry(i)
        value = at * rows + slot
        hit = lane_key == key
        fresh = first < 0
        second = jnp.where(hit & (first >= 0), value, second)
        first = jnp.where(hit & fresh, value, first)
        return first, second, jnp.where(lane == i, key, keys)

    none = jnp.full((1, links * nodes), -1, jnp.int32)
    first, second, keys = lax.fori_loop(0, links * count, collect, (none, none, none), unroll=4)

    def earlier(i, ranks_of):
        key, _, _ = entry(i)
        return ranks_of + jnp.where((keys == key) & (lane > i), 1, 0)

    rank = lax.fori_loop(0, links * count, earlier, jnp.zeros((1, links * nodes), jnp.int32), unroll=4)
    rel_y, rel_x, rel_c = ((keys & 31) >> 3) - my_y, ((keys >> 1) & 3) - my_x, (keys & 1) - my_c
    own_tab[0:1, :] = ((((rel_y & 3) << 3) + ((rel_x & 3) << 1) + (rel_c & 1)) << 1) + jnp.minimum(rank, CAP - 1)
    own_tab[1:2, :] = jnp.where(first < 0, count, first >> 3)
    own_tab[2:3, :] = jnp.where(second < 0, count, second >> 3)
    asked = jnp.where(first < 0, 0, first & 7) + (jnp.where(second < 0, 0, second & 7) << 3)
    req_out[...] = asked
    req_in[0] = asked

    others = pl.ds(1, nodes - 1)

    def wait_all(ref, sem):
        pltpu.make_async_copy(ref, ref, sem).wait()

    def exchange(blocks, buffers, received, turn):
        for s in ORDER:
            for j in range(CAP):
                buffers[s, j] = blocks(s, j)
            pltpu.make_async_remote_copy(
                src_ref=buffers.at[s], dst_ref=received.at[opposite(s)], send_sem=xy_send.at[turn],
                recv_sem=xy_recv.at[turn], device_id={"node": partner(s)}, device_id_type=MESH).start()
        for j in range(CAP):
            received[0, j] = blocks(0, j)

    def wanted(s, link):
        both = req_s[s, 0, link * nodes + opposite(s)]
        return lax.rem(both, rows), lax.div(both, rows)

    pl.semaphore_wait(entered, len(COLUMN))
    for s in ORDER:
        pltpu.make_async_remote_copy(
            src_ref=req_out, dst_ref=req_in.at[opposite(s)], send_sem=req_send, recv_sem=req_recv,
            device_id={"node": partner(s)}, device_id_type=MESH).start()
    to_scalars = [pltpu.make_async_copy(own_tab, own_s, local_sem.at[0]),
                  pltpu.make_async_copy(req_in, req_s, local_sem.at[1])]
    to_scalars[0].start()
    arrived(0, 0)
    send_tiles(0, 2)
    send_tiles(1, 1)
    for copy in local:
        copy.wait()

    def reduce(level, n):
        link = level - 1
        current = rs_v[pl.ds(level * rows + n, columns, stride), :]
        if level:
            picked = []
            for k in range(fanout):
                at = own_s[0, link * count + n * fanout + k]
                picked.append(recv_f[link][lax.div(at, CAP), lax.rem(at, CAP)])
            tiles = jnp.concatenate([off_v[link, n, k] for k in range(fanout)], axis=1)
            current = current - dot_nt(jnp.concatenate(picked, axis=1), tiles)
        return current.astype(jnp.bfloat16)

    def solve(level, n, reduced):
        return dot_nt(reduced, diag_v[level, n]).astype(jnp.bfloat16)

    def row_tiles(link, n):
        return jnp.concatenate([off_v[link, n, k] for k in range(fanout)], axis=1)

    def merge(level):
        for n in range(rows):
            merged[level - 1, n] = dot_nn(diag_v[level, n], row_tiles(level - 1, n)).astype(jnp.bfloat16)

    def answer_row(level, n, back_in):
        answer = dot_nn(back_in, diag_v[level, n])
        out_v[pl.ds(level * rows + n, columns, stride), :] = answer
        return answer.astype(jnp.bfloat16)

    def contribute(n, vector, tiles):
        products = dot_nn(vector, tiles).astype(jnp.bfloat16)
        for k in range(fanout):
            contrib[n * fanout + k] = products[:, k * size:(k + 1) * size]

    square = (rows * columns, size)
    of_row = lax.broadcasted_iota(jnp.int32, square, 0)
    of_lane = lax.broadcasted_iota(jnp.int32, square, 1)
    same_column = lax.rem(of_row, columns) == lax.rem(of_lane, columns)
    of_row = lax.div(of_row, columns)
    lane_block = lax.div(lax.broadcasted_iota(jnp.int32, (1, size), 1), columns)
    blocks = size // columns

    def choose(link):
        for start in range(0, nodes * CAP, blocks):
            owner = jnp.zeros((1, size), jnp.int32)
            for b in range(blocks):
                owner = jnp.where(lane_block == b, wanted((start + b) // CAP, link)[(start + b) % CAP], owner)
            hit = same_column & (of_row == owner)
            chosen[link, :, start * columns:start * columns + size] = jnp.where(hit, 1.0, 0.0).astype(jnp.bfloat16)

    far = (my_z + 2) % ranks
    arrivals = [(own * my_z, own * my_z + 1), (own * down, own * up + 1), (own * down + 1, own * up),
                (own * far, own * far + 1)]
    contrib[count] = jnp.zeros((columns, size), jnp.bfloat16)
    for level in range(levels):
        if level:
            wait_all(recv_f[level - 1].at[others], xy_recv.at[level - 1])
        for turn, pair in enumerate(arrivals):
            if turn > 1:
                arrived(level, turn - 1, (1,))
            reduced = [reduce(level, n) for n in pair]
            if turn > 1:
                arrived(level, turn - 1, (0,))
            for n, current in zip(pair, reduced):
                if level < links:
                    solved[level][n] = solve(level, n, current)
                else:
                    contribute(n, answer_row(level, n, solve(level, n, current)), row_tiles(level - 1, n))
        if level == 0:
            wait_all(req_in.at[others], req_recv)
            to_scalars[1].start()
            for copy in to_scalars:
                copy.wait()
        if level < links:
            exchange(lambda s, j: solved[level][wanted(s, level)[j]], send_f[level], recv_f[level], level)
            arrived(level + 1, 0)
            send_tiles(level + 1, 2)
            send_tiles(level + 2, 0)
            send_tiles(level + 2, 1)
            choose(level)
            if level:
                merge(level)

    for level in range(levels - 1, -1, -1):
        link = level - 1
        if level < links:
            wait_all(recv_b[level].at[others], xy_recv.at[links + level])

            incoming = dot_nn(chosen[level], recv_b[level][...].reshape(nodes * CAP * columns, size))
            held = solved[level][...].reshape(rows * columns, size).astype(jnp.float32)
            back_in = (held - incoming).astype(jnp.bfloat16)
            back_rows = [back_in[m * columns:(m + 1) * columns] for m in range(rows)]
            if level:
                for m in range(rows):
                    contribute(m, back_rows[m], merged[link, m])
        if level:
            exchange(lambda s, j: contrib[own_s[1 + j, link * nodes + s]], send_b[link], recv_b[link], links + link)
        if level < links:
            for m in range(rows):
                answer_row(level, m, back_rows[m])
        for c in range(columns):
            span = pl.ds(c * stride + level * rows, rows)
            pltpu.make_async_copy(out_v.at[span], out_hbm.at[span], out_sem.at[level]).start()

    for level in range(levels):
        wait_all(out_v.at[pl.ds(0, columns * rows)], out_sem.at[level])
    for s in ORDER:
        wait_all(req_in.at[s], req_send)
    for link in range(links):
        wait_all(send_f[link].at[others], xy_send.at[link])
        wait_all(send_b[link].at[others], xy_send.at[links + link])
    for level in range(levels):
        for kind, way in pieces(level):
            for step in range(3):
                tile_copy(kind, level, way, step).wait_send()


def on_device(right_side, diag_tiles, off_tiles, src_part, src_slot):
    columns, levels, rows, size = right_side.shape
    links, own, fanout = off_tiles.shape[:3]
    nodes, ranks = lax.axis_size("node"), lax.axis_size("rhs")
    dims = (columns, levels, rows, size, fanout, nodes, ranks)
    bf16 = jnp.bfloat16
    block = (columns, size)
    lanes = links * nodes
    scratch = [
        pltpu.VMEM((columns * levels * rows, size), jnp.float32),
        pltpu.VMEM((columns * levels * rows, size), jnp.float32),
        pltpu.VMEM((levels, rows, size, size), bf16),
        pltpu.VMEM((links, rows, fanout, size, size), bf16),
        pltpu.VMEM((rows * fanout + 1,) + block, bf16),
        pltpu.VMEM((links, rows * columns, nodes * CAP * columns), bf16),
        pltpu.VMEM((links - 1, rows, size, fanout * size), bf16),
        pltpu.VMEM((1, lanes), jnp.int32),
        pltpu.VMEM((nodes, 1, lanes), jnp.int32),
        pltpu.VMEM((8, lanes), jnp.int32),
    ]
    scratch += [pltpu.VMEM((rows,) + block, bf16)] * links
    scratch += [pltpu.VMEM((nodes, CAP) + block, bf16)] * (4 * links)
    scratch += [
        pltpu.SMEM((links, fanout, rows), jnp.int32),
        pltpu.SMEM((links, fanout, rows), jnp.int32),
        pltpu.SMEM((nodes, 1, lanes), jnp.int32),
        pltpu.SMEM((8, lanes), jnp.int32),
        pltpu.SemaphoreType.REGULAR,
        pltpu.SemaphoreType.DMA((levels,)),
        pltpu.SemaphoreType.DMA((5,)),
        pltpu.SemaphoreType.DMA,
        pltpu.SemaphoreType.DMA,
        pltpu.SemaphoreType.DMA((2 * links,)),
        pltpu.SemaphoreType.DMA((2 * links,)),
        pltpu.SemaphoreType.DMA((levels * 12,)),
        pltpu.SemaphoreType.DMA((levels * 12,)),
    ]
    hbm = pl.BlockSpec(memory_space=pltpu.MemorySpace.HBM)
    out = pl.pallas_call(
        functools.partial(kernel, dims),
        out_shape=jax.ShapeDtypeStruct((columns * levels * rows, size), jnp.float32),
        in_specs=[hbm] * 5,
        out_specs=hbm,
        scratch_shapes=scratch,
        compiler_params=pltpu.CompilerParams(
            collective_id=0, has_side_effects=True, vmem_limit_bytes=67043328),
    )(src_part.transpose(0, 2, 1), src_slot.transpose(0, 2, 1),
      right_side.reshape(columns * levels * rows, size), diag_tiles, off_tiles)
    return out.reshape(columns, levels, rows, size)


def solution(mesh):
    placed = (
        P("rhs", None, "node", None),
        P(None, ("node", "rhs"), None, None),
        P(None, ("node", "rhs"), None, None, None),
        P(None, "node", None),
        P(None, "node", None),
    )
    return jax.shard_map(
        on_device,
        mesh=mesh,
        in_specs=placed,
        out_specs=P("rhs", None, "node", None),
        check_vma=False,
    )
```
